32 devices in a mesh: grp: 2 (over x), chan: 16 (over z, y, core).
Axes of the slice: x: 2, y: 2, z: 4, core: 2. Of those that a mesh axis runs over, the one named last changes fastest.
Arguments:
- spectra: bfloat16 [128, 4, 2, 4096], P(('grp', 'chan')), parts along dimension 0, may hold values from -60 to 60
- valid: int32 [128, 4], P(('grp', 'chan')), parts along dimension 0, may hold values 0 or 1
- partner: int32 [16], replicated, may hold values from 0 to 15, as said below
- pair_bin: int32 [1024], P(('grp', 'chan')), parts along dimension 0, may hold values from -1 to 127, as said below
- pair_count: int32 [32], P(('grp', 'chan')), parts along dimension 0, may hold values from 24 to 32
Outputs:
- stacked: float32 [256, 1024], P(('grp', 'chan')), parts along dimension 0
The draws below stay inside these ranges and needn't reach their ends.
There are 2 independent parts, one for each index of `grp`. The reference program is written for one: setup_inputs(seed, part) draws one part's arguments, and reference() takes and returns one part's arrays. A program takes and returns all parts, laid end to end along the dimension named above; an argument that names none is the same for every part. Nothing has to cross between parts.
Inputs may be any that keep to these rules, and one draw needn't show every extreme that they name: partner[p] = p XOR r for one r of 1 to 15, the same for every p. `pair_bin`: -1 marks a row without bin, and every row pairing a channel with itself is -1; bin k is owned by block k // 8.
All inputs are finite; a program needn't handle non-finite values. No bound on the sum of `valid` on one device may be relied on, other than what follows from the above.
Results may differ from the reference program's by a relative error of at most 0.0056.
Values may be sent and summed in bfloat16 or wider, within the bound.
A program may use at most 128 MiB of HBM per device.

```python
import math
import jax
import jax.numpy as jnp
from jax import lax

CH_DEV = 4
WIN = 4
F = 4096
BAND = 128
LAGS = 1024
BINS_DEV = 8
PAIRS_DEV = 32
CHANNELS = 64
BINS = 128
N_CHAN = 16


def draw_spectra(key, part):
    nchan = CH_DEV * N_CHAN
    key_base, key_level = jax.random.split(key)
    shape = (nchan, WIN, 2, F // BAND, BAND)
    base = jnp.clip(jax.random.normal(key_base, shape, jnp.float32), -6.0, 6.0)
    levels = jax.random.uniform(key_level, (nchan, WIN, 1, F // BAND, 1), jnp.float32, 0.0, math.log(10.0))
    values = base * jnp.exp(levels)
    return values.reshape(nchan, WIN, 2, F).astype(jnp.bfloat16)


def draw_partner(key, part):
    offset = jax.random.randint(key, (), 1, N_CHAN, dtype=jnp.int32)
    return jnp.bitwise_xor(jnp.arange(N_CHAN, dtype=jnp.int32), offset)


def draw_pair_bin(key, part):
    total = PAIRS_DEV * N_CHAN
    index = jnp.arange(total, dtype=jnp.int32)
    block = index // PAIRS_DEV
    within = index % PAIRS_DEV
    square = CH_DEV * CH_DEV
    first = within % square // CH_DEV
    second = within % CH_DEV
    itself = (within < square) & (first == second)
    key_reach, key_slot = jax.random.split(key)
    distance = jax.random.randint(key_reach, (total,), 0, N_CHAN, dtype=jnp.int32)
    distance = jnp.where(within == 1, N_CHAN - 1, distance)
    distance = jnp.where(within == 2, N_CHAN // 2, distance)
    slot = jax.random.randint(key_slot, (total,), 0, BINS_DEV, dtype=jnp.int32)
    bins = (block + distance) % N_CHAN * BINS_DEV + slot
    return jnp.where(itself, -1, bins).astype(jnp.int32)


def draw_pair_count(key, part):
    lowest = PAIRS_DEV * 3 // 4
    key_count, key_high, key_step = jax.random.split(key, 3)
    counts = jax.random.randint(key_count, (N_CHAN,), lowest, PAIRS_DEV + 1, dtype=jnp.int32)
    high_at = jax.random.randint(key_high, (), 0, N_CHAN, dtype=jnp.int32)
    low_at = (high_at + jax.random.randint(key_step, (), 1, N_CHAN, dtype=jnp.int32)) % N_CHAN
    index = jnp.arange(N_CHAN, dtype=jnp.int32)
    counts = jnp.where(index == high_at, PAIRS_DEV, counts)
    counts = jnp.where(index == low_at, lowest, counts)
    return counts.astype(jnp.int32)


def set_ends(result, key, smallest, largest):
    dims = result.shape
    spot = [jax.random.randint(jax.random.fold_in(key, axis), (), 0, dims[axis]) for axis in range(len(dims))]
    result = result.at[tuple(spot)].set(smallest)
    longest = dims.index(max(dims))
    spot[longest] = (spot[longest] + 1) % dims[longest]
    return result.at[tuple(spot)].set(largest)


def setup_inputs(seed: int = 0, part: int = 0) -> dict:
    seeds = jax.random.split(jax.random.key(seed), 6)
    part_splits = jax.random.split(jax.random.fold_in(seeds[5], part), 6)
    return {
        "spectra": draw_spectra(jax.random.fold_in(jax.random.fold_in(seeds[5], part), 71), part),
        "valid": set_ends((jax.random.randint(part_splits[1], (CHANNELS, WIN), 0, 4) < 3).astype(jnp.int32), jax.random.fold_in(part_splits[1], 1), 0, 1),
        "partner": draw_partner(jax.random.fold_in(seeds[5], 71), part),
        "pair_bin": draw_pair_bin(jax.random.fold_in(jax.random.fold_in(seeds[5], part), 71), part),
        "pair_count": draw_pair_count(jax.random.fold_in(jax.random.fold_in(seeds[5], part), 71), part),
    }


def whiten(spectra, valid):
    values = spectra.astype(jnp.float32)
    power = values[:, :, 0] * values[:, :, 0] + values[:, :, 1] * values[:, :, 1]
    nchan, nwin, nfreq = power.shape
    banded = lax.optimization_barrier(jnp.mean(power.reshape(nchan, nwin, nfreq // BAND, BAND), axis=-1))
    amplitude = jnp.repeat(jnp.sqrt(banded + 1e-06), BAND, axis=-1)
    weights = valid.astype(jnp.float32)[:, :, None, None]
    return (values * weights / amplitude[:, :, None, :]).astype(jnp.bfloat16)

def lag_table():
    freqs = jnp.arange(F, dtype=jnp.int32)
    shifts = jnp.arange(LAGS, dtype=jnp.int32) - LAGS // 2
    phase = jnp.mod(freqs[:, None] * shifts[None, :], 2 * F)
    angle = phase.astype(jnp.float32) * (2.0 * math.pi / (2 * F))
    scale = 1.0 / math.sqrt(F)
    return jnp.concatenate([jnp.cos(angle) * scale, -jnp.sin(angle) * scale], axis=0).astype(jnp.bfloat16)

def correlate(own_block, other_block, table):
    own_real = own_block[:, :, 0].astype(jnp.float32)
    own_imag = own_block[:, :, 1].astype(jnp.float32)
    oth_real = other_block[:, :, 0].astype(jnp.float32)
    oth_imag = other_block[:, :, 1].astype(jnp.float32)
    real_part = jnp.einsum('awf,bwf->abf', own_real, oth_real) + jnp.einsum('awf,bwf->abf', own_imag, oth_imag)
    imag_part = jnp.einsum('awf,bwf->abf', own_imag, oth_real) - jnp.einsum('awf,bwf->abf', own_real, oth_imag)
    nchan = own_block.shape[0]
    nwin = own_block.shape[1]
    spec = (jnp.concatenate([real_part, imag_part], axis=-1) * (1.0 / nwin)).reshape(nchan * nchan, -1)
    spec = spec.astype(jnp.bfloat16)
    return jnp.dot(spec, table, preferred_element_type=jnp.float32)

def reference(spectra, valid, partner, pair_bin, pair_count):
    white = whiten(spectra, valid)
    blocks = white.reshape(N_CHAN, CH_DEV, WIN, 2, F)
    table = lag_table()

    def one_block(block_index):
        own_block = lax.dynamic_index_in_dim(blocks, block_index, 0, keepdims=False)
        other_index = lax.dynamic_index_in_dim(partner, block_index, 0, keepdims=False)
        other_block = lax.dynamic_index_in_dim(blocks, other_index, 0, keepdims=False)
        return jnp.concatenate([correlate(own_block, own_block, table), correlate(own_block, other_block, table)], axis=0)
    corr_all = lax.map(one_block, jnp.arange(N_CHAN, dtype=jnp.int32))
    bins = pair_bin.reshape(N_CHAN, PAIRS_DEV)
    rows = jnp.arange(PAIRS_DEV, dtype=jnp.int32)
    keep = (rows[None, :] < pair_count[:, None]) & (bins >= 0)
    segment = jnp.where(keep, bins, BINS).reshape(-1)
    summed = jax.ops.segment_sum(corr_all.reshape(-1, LAGS), segment, num_segments=BINS + 1)[:BINS]
    return summed * (1.0 / math.sqrt(PAIRS_DEV // BINS_DEV))
```

```python
import functools
import math

import jax
import jax.numpy as jnp
import ml_dtypes
import numpy as np
from jax import lax
from jax.experimental import pallas as pl
from jax.experimental.pallas import tpu as pltpu
from jax.sharding import PartitionSpec as P

F = 4096
BAND = 128
LAGS = 1024
BINS_DEV = 8
PAIRS_DEV = 32
LANES = 128


def from_partner(block, axis, bit):
    count = lax.axis_size(axis)
    route = []
    for low in range(count):
        high = low | 1 << bit
        if high != low and high < count:
            route += [(low, high), (high, low)]
    return lax.ppermute(block, axis, route)


def whiten(spectra, valid):
    values = spectra.astype(jnp.float32)
    power = values[:, :, 0] * values[:, :, 0] + values[:, :, 1] * values[:, :, 1]
    nchan, nwin, nfreq = power.shape
    banded = jnp.mean(power.reshape(nchan, nwin, nfreq // BAND, BAND), axis=-1)
    amplitude = jnp.repeat(jnp.sqrt(banded + 1e-06), BAND, axis=-1)
    weights = valid.astype(jnp.float32)[:, :, None, None]
    return (values * weights / amplitude[:, :, None, :]).astype(jnp.bfloat16)


def lag_table():
    freqs = jnp.arange(F, dtype=jnp.int32)
    shifts = jnp.arange(LAGS, dtype=jnp.int32) - LAGS // 2
    phase = jnp.mod(freqs[:, None] * shifts[None, :], 2 * F)
    angle = phase.astype(jnp.float32) * (2.0 * math.pi / (2 * F))
    scale = 1.0 / math.sqrt(F)
    return jnp.concatenate([jnp.cos(angle) * scale, -jnp.sin(angle) * scale], axis=0).astype(
        jnp.bfloat16
    )


def cross_product(left_part, right_part):
    return jnp.einsum("awf,bwf->abf", left_part, right_part, preferred_element_type=jnp.float32)


def correlate(own_block, other_block, table):
    own_real = own_block[:, :, 0]
    own_imag = own_block[:, :, 1]
    oth_real = other_block[:, :, 0]
    oth_imag = other_block[:, :, 1]
    real_part = cross_product(own_real, oth_real) + cross_product(own_imag, oth_imag)
    imag_part = cross_product(own_imag, oth_real) - cross_product(own_real, oth_imag)
    nchan = own_block.shape[0]
    nwin = own_block.shape[1]
    spec = (jnp.concatenate([real_part, imag_part], axis=-1) * (1.0 / nwin)).reshape(
        nchan * nchan, -1
    )
    spec = spec.astype(jnp.bfloat16)
    return jnp.dot(spec, table, preferred_element_type=jnp.float32)


def select_sum(selector, corr_high, corr_low):
    return jnp.dot(selector, corr_high, preferred_element_type=jnp.float32) + jnp.dot(
        selector, corr_low, preferred_element_type=jnp.float32
    )


def on_device_blocks(spectra, valid, partner, pair_bin, pair_count):
    white = whiten(spectra, valid)
    nblocks = lax.axis_size("chan")
    round_mask = partner[0]
    paired = white
    for bit_index in range(nblocks.bit_length() - 1):
        swapped = from_partner(paired, "chan", bit_index)
        paired = jnp.where(round_mask >> bit_index & 1 == 1, swapped, paired)
    table = lag_table()
    self_corr = correlate(white, white, table)
    cross_corr = correlate(white, paired, table)
    corr = jnp.concatenate([self_corr, cross_corr], axis=0)
    corr_high = corr.astype(jnp.bfloat16)
    corr_low = (corr - corr_high.astype(jnp.float32)).astype(jnp.bfloat16)
    rows = jnp.arange(corr.shape[0], dtype=jnp.int32)
    live_rows = (rows < pair_count[0]) & (pair_bin >= 0)
    kept_bins = jnp.where(live_rows, pair_bin, -1)
    targets = lax.iota(jnp.int32, nblocks * BINS_DEV)
    selector = (kept_bins[None, :] == targets[:, None]).astype(jnp.bfloat16)
    terms = select_sum(selector, corr_high, corr_low).reshape(nblocks, BINS_DEV, -1)
    received = lax.all_to_all(terms, "chan", split_axis=0, concat_axis=0, tiled=True)
    summed = jnp.sum(received, axis=0)
    return summed * (1.0 / math.sqrt(PAIRS_DEV // BINS_DEV))


def base_table(nfreq):
    shifts = np.arange(LAGS) - LAGS // 2
    angle = np.mod(np.arange(nfreq)[:, None] * shifts[None, :], 2 * F) * (2.0 * math.pi / (2 * F))
    cos, sin = np.cos(angle), np.sin(angle)
    return np.concatenate(
        [np.concatenate([cos, sin], axis=1), np.concatenate([-sin, cos], axis=1)], axis=0
    ).astype(ml_dtypes.bfloat16)


def slice_phases(nslices, nfreq, scale):
    shifts = np.arange(LAGS) - LAGS // 2
    first = np.arange(nslices) * nfreq
    angle = np.mod(first[:, None] * shifts[None, :], 2 * F) * (2.0 * math.pi / (2 * F))
    both = np.concatenate([np.cos(angle), -np.sin(angle)], axis=1) * scale
    return both.astype(np.float32)[:, None, :]


def expanders(nchan, nwin):
    row = np.arange(LANES)
    per_chan = 2 * nwin
    step = row // (nchan * per_chan)
    first = row // per_chan % nchan
    window = row // 2 % nwin
    second = (first + step) % nchan
    nvalid = nchan * nwin
    pair = first * nchan + second
    lanes = (
        nvalid + pair,
        nvalid + nchan * nchan + pair,
        first * nwin + window,
        second * nwin + window,
    )
    return np.concatenate(
        [(np.arange(LANES)[:, None] == lane[None, :]) for lane in lanes], axis=1
    ).astype(ml_dtypes.bfloat16)


def swap_pairs(rows):
    size = rows.shape[-2]
    axis = rows.ndim - 2
    even = lax.broadcasted_iota(jnp.int32, rows.shape, axis) % 2 == 0
    return jnp.where(
        even, pltpu.roll(rows, size - 1, axis), pltpu.roll(rows, 1, axis)
    ), even


def kernel(
    dims,
    partner_ref,
    spectra_ref,
    meta_ref,
    expand_ref,
    table_hbm,
    phase_hbm,
    out_ref,
    raw,
    metas,
    table,
    phases,
    rolled,
    turned,
    kept,
    other_valid,
    selector,
    products,
    outgoing,
    incoming,
    local_sems,
    send_a,
    recv_a,
    send_m,
    recv_m,
    send_b,
    recv_b,
):
    n, nchan, nwin, nfreq, nbins_dev = dims
    nrow = nchan * nwin * 2
    nbins = n * nbins_dev
    me = lax.axis_index("chan")
    copy_table = pltpu.make_async_copy(table_hbm, table, local_sems.at[0])
    copy_phase = pltpu.make_async_copy(phase_hbm, phases, local_sems.at[1])

    def mine(target):
        return pl.ds(pl.multiple_of(target * nfreq, nfreq), nfreq)

    own_raw = pltpu.make_async_copy(spectra_ref.at[:, mine(me)], raw.at[me], local_sems.at[2])
    own_meta = pltpu.make_async_copy(meta_ref, metas.at[me], local_sems.at[3])

    barrier = pltpu.get_barrier_semaphore()
    for k in range(1, n):
        pl.semaphore_signal(
            barrier,
            inc=1,
            device_id={"chan": lax.rem(me + k, n)},
            device_id_type=pl.DeviceIdType.MESH,
        )
    own_raw.start()
    own_meta.start()
    copy_table.start()
    copy_phase.start()
    pl.semaphore_wait(barrier, n - 1)

    def remote(src, dst, send, recv, target):
        return pltpu.make_async_remote_copy(
            src_ref=src,
            dst_ref=dst,
            send_sem=send,
            recv_sem=recv,
            device_id={"chan": target},
            device_id_type=pl.DeviceIdType.MESH,
        )

    def meta_copy(k, source):
        return remote(
            meta_ref, metas.at[source], send_m.at[k], recv_m.at[k], lax.rem(me + k, n)
        )

    def raw_copy(k, source):
        target = lax.rem(me + k, n)
        return remote(
            spectra_ref.at[:, mine(target)], raw.at[source], send_a.at[k], recv_a.at[k], target
        )

    order = sorted(range(1, n), key=lambda k: -min(k, n - k))
    for k in order:
        meta_copy(k, me).start()
    for k in order:
        raw_copy(k, me).start()

    own_meta.wait()
    for k in range(1, n):
        meta_copy(k, lax.rem(me + n - k, n)).wait_recv()
    values = metas[:, 0, :]
    lane = lax.broadcasted_iota(jnp.int32, (n, LANES), 1)
    nvalid = nchan * nwin
    npairs = 2 * nchan * nchan
    is_count = lane == nvalid + npairs
    count = jnp.sum(jnp.where(is_count, values, 0), axis=1, keepdims=True)
    is_pair = (lane >= nvalid) & (lane < nvalid + npairs)
    dropped = is_pair & ((lane - nvalid >= count) | (values < 0))
    values = jnp.where(dropped, -1, jnp.where(is_count, 0, values))
    spread = jnp.dot(
        values.astype(jnp.float32).astype(jnp.bfloat16),
        expand_ref[...],
        preferred_element_type=jnp.float32,
    )
    self_bin = spread[:, :LANES]
    cross_bin = spread[:, LANES : 2 * LANES]
    first_ok = spread[:, 2 * LANES : 3 * LANES] > 0.5
    second_valid = spread[:, 3 * LANES :]
    self_bin = jnp.where(first_ok & (second_valid > 0.5), self_bin, -1.0)
    cross_bin = jnp.where(first_ok, cross_bin, -1.0)
    for p in range(n):
        kept[p, 0:1, :] = self_bin[p : p + 1]
        kept[p, 1:2, :] = cross_bin[p : p + 1]
        other_valid[p, 0:1, :] = second_valid[p : p + 1]

    bin_rows = lax.broadcasted_iota(jnp.int32, (nbins, LANES), 0).astype(jnp.float32)

    def select(p, carry):
        other = other_valid[partner_ref[p], 0:1, :]
        crossing = jnp.where(other > 0.5, kept[p, 1:2, :], -1.0)
        at = pl.multiple_of(p * 2 * LANES, 2 * LANES)
        own = kept[p, 0:1, :]
        selector[:, pl.ds(at, LANES)] = jnp.where(bin_rows == own, 1.0, 0.0).astype(jnp.bfloat16)
        selector[:, pl.ds(at + LANES, LANES)] = jnp.where(bin_rows == crossing, 1.0, 0.0).astype(
            jnp.bfloat16
        )
        return carry

    lax.fori_loop(0, n, select, 0)

    def prepare(p):
        x = raw[p].astype(jnp.float32).reshape(nchan, 2 * nwin, nfreq)
        swapped, even = swap_pairs(x)
        power = x * x + swapped * swapped
        scales = []
        for b in range(nfreq // BAND):
            total = jnp.sum(power[:, :, b * BAND : (b + 1) * BAND], axis=-1, keepdims=True)
            scale = lax.rsqrt(total * (1.0 / BAND) + 1e-06)
            scales.append(jnp.broadcast_to(scale, (nchan, 2 * nwin, BAND)))
        scale = jnp.concatenate(scales, axis=-1)
        white = x * scale
        turn = jnp.where(even, -swapped, swapped) * scale
        for s in range(nchan):
            at = s * nrow
            part = jnp.concatenate([white[s:], white[:s]], axis=0) if s else white
            rolled[p, at : at + nrow, :] = part.reshape(nrow, nfreq).astype(jnp.bfloat16)
            part = jnp.concatenate([turn[s:], turn[:s]], axis=0) if s else turn
            turned[p, at : at + nrow, :] = part.reshape(nrow, nfreq).astype(jnp.bfloat16)

    own_raw.wait()
    prepare(me)

    def arrive(i, carry):
        k = lax.rem(i, n)
        source = lax.rem(me + n - k, n)
        raw_copy(k, source).wait_recv()
        prepare(source)
        return carry

    lax.fori_loop(1, n, arrive, 0)

    def multiply(p, carry):
        q = partner_ref[p]
        x = rolled[p, 0:nrow, :]
        at = pl.multiple_of(p * 2 * LANES, 2 * LANES)
        for s in range(nchan):
            here = slice(s * nrow, (s + 1) * nrow)
            mid = at + s * nrow
            products[pl.ds(mid, nrow), 0:nfreq] = x * rolled[p, here, :]
            products[pl.ds(mid, nrow), nfreq : 2 * nfreq] = x * turned[p, here, :]
            products[pl.ds(mid + LANES, nrow), 0:nfreq] = x * rolled[q, here, :]
            products[pl.ds(mid + LANES, nrow), nfreq : 2 * nfreq] = x * turned[q, here, :]
        return carry

    lax.fori_loop(0, n, multiply, 0)

    terms = jnp.dot(selector[...], products[...], preferred_element_type=jnp.float32)
    outgoing[...] = terms.reshape(n, nbins_dev, 2 * nfreq).astype(jnp.bfloat16)

    def term_copy(k, source):
        target = lax.rem(me + k, n)
        return remote(
            outgoing.at[target], incoming.at[source], send_b.at[k], recv_b.at[k], target
        )

    own_terms = pltpu.make_async_copy(outgoing.at[me], incoming.at[me], local_sems.at[4])
    for k in order:
        term_copy(k, me).start()
    own_terms.start()
    copy_table.wait()
    copy_phase.wait()
    own_terms.wait()
    for k in range(1, n):
        term_copy(k, lax.rem(me + n - k, n)).wait_recv()

    stacked = incoming[...].astype(jnp.float32).reshape(nbins, 2 * nfreq).astype(jnp.bfloat16)
    lags = jnp.dot(stacked, table[...], preferred_element_type=jnp.float32)
    lags = jnp.sum(lags.reshape(n, nbins_dev, 2 * LAGS) * phases[...], axis=0)
    out_ref[...] = lags[:, :LAGS] + lags[:, LAGS:]

    for k in range(1, n):
        meta_copy(k, me).wait_send()
        raw_copy(k, me).wait_send()
        term_copy(k, me).wait_send()


def on_device_slices(spectra, valid, partner, pair_bin, pair_count):
    n = lax.axis_size("chan")
    nchan, nwin, _, nfreq_all = spectra.shape
    nfreq = nfreq_all // n
    nrow = nchan * nwin * 2
    nbins = n * BINS_DEV
    scale = 1.0 / (math.sqrt(nfreq_all) * nwin * math.sqrt(PAIRS_DEV // BINS_DEV))
    lanes = jnp.concatenate([valid.reshape(-1), pair_bin, pair_count])
    lanes = jnp.pad(lanes, (0, LANES - lanes.shape[0]))
    meta = jnp.broadcast_to(lanes[None, :], (8, LANES))
    hbm = pl.BlockSpec(memory_space=pl.ANY)
    vmem = pl.BlockSpec(memory_space=pltpu.VMEM)
    dma = pltpu.SemaphoreType.DMA
    return pl.pallas_call(
        functools.partial(kernel, (n, nchan, nwin, nfreq, BINS_DEV)),
        out_shape=jax.ShapeDtypeStruct((BINS_DEV, LAGS), jnp.float32),
        in_specs=[pl.BlockSpec(memory_space=pltpu.SMEM), hbm, hbm, vmem, hbm, hbm],
        out_specs=vmem,
        scratch_shapes=[
            pltpu.VMEM((n, nrow, nfreq), jnp.bfloat16),
            pltpu.VMEM((n, 8, LANES), jnp.int32),
            pltpu.VMEM((2 * nfreq, 2 * LAGS), jnp.bfloat16),
            pltpu.VMEM((n, 1, 2 * LAGS), jnp.float32),
            pltpu.VMEM((n, nchan * nrow, nfreq), jnp.bfloat16),
            pltpu.VMEM((n, nchan * nrow, nfreq), jnp.bfloat16),
            pltpu.VMEM((n, 8, LANES), jnp.float32),
            pltpu.VMEM((n, 8, LANES), jnp.float32),
            pltpu.VMEM((nbins, n * 2 * LANES), jnp.bfloat16),
            pltpu.VMEM((n * 2 * LANES, 2 * nfreq), jnp.bfloat16),
            pltpu.VMEM((n, BINS_DEV, 2 * nfreq), jnp.bfloat16),
            pltpu.VMEM((n, BINS_DEV, 2 * nfreq), jnp.bfloat16),
            dma((5,)),
            dma((n,)),
            dma((n,)),
            dma((n,)),
            dma((n,)),
            dma((n,)),
            dma((n,)),
        ],
        compiler_params=pltpu.CompilerParams(
            collective_id=0, has_side_effects=True, vmem_limit_bytes=40 * 1024 * 1024
        ),
    )(
        partner,
        spectra.reshape(nrow, nfreq_all),
        meta,
        jnp.asarray(expanders(nchan, nwin)),
        jnp.asarray(base_table(nfreq)),
        jnp.asarray(slice_phases(n, nfreq, scale)),
    )


def solution(mesh):
    in_specs = (
        P(("grp", "chan"), None, None, None),
        P(("grp", "chan"), None),
        P(),
        P(("grp", "chan")),
        P(("grp", "chan")),
    )
    out_specs = P(("grp", "chan"), None)
    whole_bands = F % (mesh.shape["chan"] * BAND) == 0
    return jax.shard_map(
        on_device_slices if whole_bands else on_device_blocks,
        mesh=mesh,
        in_specs=in_specs,
        out_specs=out_specs,
        check_vma=False,
    )
```

```python
import functools
import math

import jax
import jax.numpy as jnp
import ml_dtypes
import numpy as np
from jax import lax
from jax.experimental import pallas as pl
from jax.experimental.pallas import tpu as pltpu
from jax.sharding import PartitionSpec as P

F = 4096
BAND = 128
LAGS = 1024
BINS_DEV = 8
PAIRS_DEV = 32
LANES = 128


def from_partner(block, axis, bit):
    count = lax.axis_size(axis)
    route = []
    for low in range(count):
        high = low | 1 << bit
        if high != low and high < count:
            route += [(low, high), (high, low)]
    return lax.ppermute(block, axis, route)


def whiten(spectra, valid):
    values = spectra.astype(jnp.float32)
    power = values[:, :, 0] * values[:, :, 0] + values[:, :, 1] * values[:, :, 1]
    nchan, nwin, nfreq = power.shape
    banded = jnp.mean(power.reshape(nchan, nwin, nfreq // BAND, BAND), axis=-1)
    amplitude = jnp.repeat(jnp.sqrt(banded + 1e-06), BAND, axis=-1)
    weights = valid.astype(jnp.float32)[:, :, None, None]
    return (values * weights / amplitude[:, :, None, :]).astype(jnp.bfloat16)


def lag_table():
    freqs = jnp.arange(F, dtype=jnp.int32)
    shifts = jnp.arange(LAGS, dtype=jnp.int32) - LAGS // 2
    phase = jnp.mod(freqs[:, None] * shifts[None, :], 2 * F)
    angle = phase.astype(jnp.float32) * (2.0 * math.pi / (2 * F))
    scale = 1.0 / math.sqrt(F)
    return jnp.concatenate([jnp.cos(angle) * scale, -jnp.sin(angle) * scale], axis=0).astype(
        jnp.bfloat16
    )


def cross_product(left_part, right_part):
    return jnp.einsum("awf,bwf->abf", left_part, right_part, preferred_element_type=jnp.float32)


def correlate(own_block, other_block, table):
    own_real = own_block[:, :, 0]
    own_imag = own_block[:, :, 1]
    oth_real = other_block[:, :, 0]
    oth_imag = other_block[:, :, 1]
    real_part = cross_product(own_real, oth_real) + cross_product(own_imag, oth_imag)
    imag_part = cross_product(own_imag, oth_real) - cross_product(own_real, oth_imag)
    nchan = own_block.shape[0]
    nwin = own_block.shape[1]
    spec = (jnp.concatenate([real_part, imag_part], axis=-1) * (1.0 / nwin)).reshape(
        nchan * nchan, -1
    )
    spec = spec.astype(jnp.bfloat16)
    return jnp.dot(spec, table, preferred_element_type=jnp.float32)


def select_sum(selector, corr_high, corr_low):
    return jnp.dot(selector, corr_high, preferred_element_type=jnp.float32) + jnp.dot(
        selector, corr_low, preferred_element_type=jnp.float32
    )


def on_device_blocks(spectra, valid, partner, pair_bin, pair_count):
    white = whiten(spectra, valid)
    nblocks = lax.axis_size("chan")
    round_mask = partner[0]
    paired = white
    for bit_index in range(nblocks.bit_length() - 1):
        swapped = from_partner(paired, "chan", bit_index)
        paired = jnp.where(round_mask >> bit_index & 1 == 1, swapped, paired)
    table = lag_table()
    self_corr = correlate(white, white, table)
    cross_corr = correlate(white, paired, table)
    corr = jnp.concatenate([self_corr, cross_corr], axis=0)
    corr_high = corr.astype(jnp.bfloat16)
    corr_low = (corr - corr_high.astype(jnp.float32)).astype(jnp.bfloat16)
    rows = jnp.arange(corr.shape[0], dtype=jnp.int32)
    live_rows = (rows < pair_count[0]) & (pair_bin >= 0)
    kept_bins = jnp.where(live_rows, pair_bin, -1)
    targets = lax.iota(jnp.int32, nblocks * BINS_DEV)
    selector = (kept_bins[None, :] == targets[:, None]).astype(jnp.bfloat16)
    terms = select_sum(selector, corr_high, corr_low).reshape(nblocks, BINS_DEV, -1)
    received = lax.all_to_all(terms, "chan", split_axis=0, concat_axis=0, tiled=True)
    summed = jnp.sum(received, axis=0)
    return summed * (1.0 / math.sqrt(PAIRS_DEV // BINS_DEV))


def base_table(nfreq):
    shifts = np.arange(LAGS) - LAGS // 2
    angle = np.mod(np.arange(nfreq)[:, None] * shifts[None, :], 2 * F) * (2.0 * math.pi / (2 * F))
    cos, sin = np.cos(angle), np.sin(angle)
    return np.concatenate(
        [np.concatenate([cos, sin], axis=1), np.concatenate([-sin, cos], axis=1)], axis=0
    ).astype(ml_dtypes.bfloat16)


def slice_phases(nslices, nfreq, scale):
    shifts = np.arange(LAGS) - LAGS // 2
    first = np.arange(nslices) * nfreq
    angle = np.mod(first[:, None] * shifts[None, :], 2 * F) * (2.0 * math.pi / (2 * F))
    both = np.concatenate([np.cos(angle), -np.sin(angle)], axis=1) * scale
    return both.astype(np.float32)[:, None, :]


def expanders(nchan, nwin):
    row = np.arange(LANES)
    per_chan = 2 * nwin
    step = row // (nchan * per_chan)
    first = row // per_chan % nchan
    window = row // 2 % nwin
    second = (first + step) % nchan
    nvalid = nchan * nwin
    pair = first * nchan + second
    lanes = (
        nvalid + pair,
        nvalid + nchan * nchan + pair,
        first * nwin + window,
        second * nwin + window,
    )
    return np.concatenate(
        [(np.arange(LANES)[:, None] == lane[None, :]) for lane in lanes], axis=1
    ).astype(ml_dtypes.bfloat16)


def swap_pairs(rows):
    size = rows.shape[-2]
    axis = rows.ndim - 2
    even = lax.broadcasted_iota(jnp.int32, rows.shape, axis) % 2 == 0
    return jnp.where(
        even, pltpu.roll(rows, size - 1, axis), pltpu.roll(rows, 1, axis)
    ), even


def kernel(
    dims,
    spectra_ref,
    valid_hbm,
    partner_hbm,
    bin_hbm,
    count_hbm,
    expand_hbm,
    table_hbm,
    phase_hbm,
    out_ref,
    valid_ref,
    partner_ref,
    bin_ref,
    count_ref,
    expand_ref,
    meta_ref,
    raw,
    metas,
    table,
    phases,
    rolled,
    turned,
    kept,
    other_valid,
    selector,
    products,
    outgoing,
    incoming,
    local_sems,
    send_a,
    recv_a,
    send_m,
    recv_m,
    send_b,
    recv_b,
):
    n, nchan, nwin, nfreq, nbins_dev = dims
    nrow = nchan * nwin * 2
    nbins = n * nbins_dev
    me = lax.axis_index("chan")
    copy_table = pltpu.make_async_copy(table_hbm, table, local_sems.at[0])
    copy_phase = pltpu.make_async_copy(phase_hbm, phases, local_sems.at[1])

    def mine(target):
        return pl.ds(pl.multiple_of(target * nfreq, nfreq), nfreq)

    own_raw = pltpu.make_async_copy(
        spectra_ref.at[:, :, :, mine(me)], raw.at[me], local_sems.at[2]
    )
    own_meta = pltpu.make_async_copy(meta_ref, metas.at[me], local_sems.at[3])
    small = [
        pltpu.make_async_copy(src, dst, local_sems.at[5 + i])
        for i, (src, dst) in enumerate(
            (
                (valid_hbm, valid_ref),
                (bin_hbm, bin_ref),
                (count_hbm, count_ref),
                (partner_hbm, partner_ref),
                (expand_hbm, expand_ref),
            )
        )
    ]
    for copy in small:
        copy.start()

    barrier = pltpu.get_barrier_semaphore()
    for k in range(1, n):
        pl.semaphore_signal(
            barrier,
            inc=1,
            device_id={"chan": lax.rem(me + k, n)},
            device_id_type=pl.DeviceIdType.MESH,
        )
    own_raw.start()
    copy_table.start()
    copy_phase.start()
    for copy in small:
        copy.wait()
    lane = lax.broadcasted_iota(jnp.int32, metas.shape[1:], 1)
    meta = jnp.full(metas.shape[1:], count_ref[0], jnp.int32)
    for c in range(nchan):
        for w in range(nwin):
            meta = jnp.where(lane == c * nwin + w, valid_ref[c, w], meta)
    for row in range(2 * nchan * nchan):
        meta = jnp.where(lane == nchan * nwin + row, bin_ref[row], meta)
    meta_ref[...] = meta
    pl.semaphore_wait(barrier, n - 1)
    own_meta.start()

    def remote(src, dst, send, recv, target):
        return pltpu.make_async_remote_copy(
            src_ref=src,
            dst_ref=dst,
            send_sem=send,
            recv_sem=recv,
            device_id={"chan": target},
            device_id_type=pl.DeviceIdType.MESH,
        )

    def meta_copy(k, source):
        return remote(
            meta_ref, metas.at[source], send_m.at[k], recv_m.at[k], lax.rem(me + k, n)
        )

    def raw_copy(k, source):
        target = lax.rem(me + k, n)
        return remote(
            spectra_ref.at[:, :, :, mine(target)], raw.at[source], send_a.at[k], recv_a.at[k], target
        )

    order = sorted(range(1, n), key=lambda k: -min(k, n - k))
    for k in order:
        meta_copy(k, me).start()
    for k in order:
        raw_copy(k, me).start()

    own_meta.wait()
    for k in range(1, n):
        meta_copy(k, lax.rem(me + n - k, n)).wait_recv()
    values = metas[:, 0, :]
    lane = lax.broadcasted_iota(jnp.int32, (n, LANES), 1)
    nvalid = nchan * nwin
    npairs = 2 * nchan * nchan
    is_count = lane == nvalid + npairs
    count = jnp.sum(jnp.where(is_count, values, 0), axis=1, keepdims=True)
    is_pair = (lane >= nvalid) & (lane < nvalid + npairs)
    dropped = is_pair & ((lane - nvalid >= count) | (values < 0))
    values = jnp.where(dropped, -1, jnp.where(is_count, 0, values))
    spread = jnp.dot(
        values.astype(jnp.float32).astype(jnp.bfloat16),
        expand_ref[...],
        preferred_element_type=jnp.float32,
    )
    self_bin = spread[:, :LANES]
    cross_bin = spread[:, LANES : 2 * LANES]
    first_ok = spread[:, 2 * LANES : 3 * LANES] > 0.5
    second_valid = spread[:, 3 * LANES :]
    self_bin = jnp.where(first_ok & (second_valid > 0.5), self_bin, -1.0)
    cross_bin = jnp.where(first_ok, cross_bin, -1.0)
    for p in range(n):
        kept[p, 0:1, :] = self_bin[p : p + 1]
        kept[p, 1:2, :] = cross_bin[p : p + 1]
        other_valid[p, 0:1, :] = second_valid[p : p + 1]

    bin_rows = lax.broadcasted_iota(jnp.int32, (nbins, LANES), 0).astype(jnp.float32)

    def select(p, carry):
        other = other_valid[partner_ref[p], 0:1, :]
        crossing = jnp.where(other > 0.5, kept[p, 1:2, :], -1.0)
        at = pl.multiple_of(p * 2 * LANES, 2 * LANES)
        own = kept[p, 0:1, :]
        selector[:, pl.ds(at, LANES)] = jnp.where(bin_rows == own, 1.0, 0.0).astype(jnp.bfloat16)
        selector[:, pl.ds(at + LANES, LANES)] = jnp.where(bin_rows == crossing, 1.0, 0.0).astype(
            jnp.bfloat16
        )
        return carry

    lax.fori_loop(0, n, select, 0)

    def prepare(p):
        x = raw[p].astype(jnp.float32).reshape(nchan, 2 * nwin, nfreq)
        swapped, even = swap_pairs(x)
        power = x * x + swapped * swapped
        scales = []
        for b in range(nfreq // BAND):
            total = jnp.sum(power[:, :, b * BAND : (b + 1) * BAND], axis=-1, keepdims=True)
            scale = lax.rsqrt(total * (1.0 / BAND) + 1e-06)
            scales.append(jnp.broadcast_to(scale, (nchan, 2 * nwin, BAND)))
        scale = jnp.concatenate(scales, axis=-1)
        white = x * scale
        turn = jnp.where(even, -swapped, swapped) * scale
        for s in range(nchan):
            at = s * nrow
            part = jnp.concatenate([white[s:], white[:s]], axis=0) if s else white
            rolled[p, at : at + nrow, :] = part.reshape(nrow, nfreq).astype(jnp.bfloat16)
            part = jnp.concatenate([turn[s:], turn[:s]], axis=0) if s else turn
            turned[p, at : at + nrow, :] = part.reshape(nrow, nfreq).astype(jnp.bfloat16)

    own_raw.wait()
    prepare(me)

    def arrive(i, carry):
        k = lax.rem(i, n)
        source = lax.rem(me + n - k, n)
        raw_copy(k, source).wait_recv()
        prepare(source)
        return carry

    lax.fori_loop(1, n, arrive, 0)

    def multiply(p, carry):
        q = partner_ref[p]
        x = rolled[p, 0:nrow, :]
        at = pl.multiple_of(p * 2 * LANES, 2 * LANES)
        for s in range(nchan):
            here = slice(s * nrow, (s + 1) * nrow)
            mid = at + s * nrow
            products[pl.ds(mid, nrow), 0:nfreq] = x * rolled[p, here, :]
            products[pl.ds(mid, nrow), nfreq : 2 * nfreq] = x * turned[p, here, :]
            products[pl.ds(mid + LANES, nrow), 0:nfreq] = x * rolled[q, here, :]
            products[pl.ds(mid + LANES, nrow), nfreq : 2 * nfreq] = x * turned[q, here, :]
        return carry

    lax.fori_loop(0, n, multiply, 0)

    terms = jnp.dot(selector[...], products[...], preferred_element_type=jnp.float32)
    outgoing[...] = terms.reshape(n, nbins_dev, 2 * nfreq).astype(jnp.bfloat16)

    def term_copy(k, source):
        target = lax.rem(me + k, n)
        return remote(
            outgoing.at[target], incoming.at[source], send_b.at[k], recv_b.at[k], target
        )

    own_terms = pltpu.make_async_copy(outgoing.at[me], incoming.at[me], local_sems.at[4])
    for k in order:
        term_copy(k, me).start()
    own_terms.start()
    copy_table.wait()
    copy_phase.wait()
    own_terms.wait()
    for k in range(1, n):
        term_copy(k, lax.rem(me + n - k, n)).wait_recv()

    stacked = incoming[...].astype(jnp.float32).reshape(nbins, 2 * nfreq).astype(jnp.bfloat16)
    lags = jnp.dot(stacked, table[...], preferred_element_type=jnp.float32)
    lags = jnp.sum(lags.reshape(n, nbins_dev, 2 * LAGS) * phases[...], axis=0)
    out_ref[...] = lags[:, :LAGS] + lags[:, LAGS:]

    for k in range(1, n):
        meta_copy(k, me).wait_send()
        raw_copy(k, me).wait_send()
        term_copy(k, me).wait_send()


def on_device_slices(spectra, valid, partner, pair_bin, pair_count):
    n = lax.axis_size("chan")
    nchan, nwin, _, nfreq_all = spectra.shape
    nfreq = nfreq_all // n
    nrow = nchan * nwin * 2
    nbins = n * BINS_DEV
    scale = 1.0 / (math.sqrt(nfreq_all) * nwin * math.sqrt(PAIRS_DEV // BINS_DEV))
    hbm = pl.BlockSpec(memory_space=pltpu.HBM)
    vmem = pl.BlockSpec(memory_space=pltpu.VMEM)
    dma = pltpu.SemaphoreType.DMA
    return pl.pallas_call(
        functools.partial(kernel, (n, nchan, nwin, nfreq, BINS_DEV)),
        out_shape=jax.ShapeDtypeStruct((BINS_DEV, LAGS), jnp.float32),
        in_specs=[hbm] * 8,
        out_specs=vmem,
        scratch_shapes=[
            pltpu.SMEM(valid.shape, jnp.int32),
            pltpu.SMEM(partner.shape, jnp.int32),
            pltpu.SMEM(pair_bin.shape, jnp.int32),
            pltpu.SMEM(pair_count.shape, jnp.int32),
            pltpu.VMEM((LANES, 4 * LANES), jnp.bfloat16),
            pltpu.VMEM((8, LANES), jnp.int32),
            pltpu.VMEM((n, nchan, nwin, 2, nfreq), jnp.bfloat16),
            pltpu.VMEM((n, 8, LANES), jnp.int32),
            pltpu.VMEM((2 * nfreq, 2 * LAGS), jnp.bfloat16),
            pltpu.VMEM((n, 1, 2 * LAGS), jnp.float32),
            pltpu.VMEM((n, nchan * nrow, nfreq), jnp.bfloat16),
            pltpu.VMEM((n, nchan * nrow, nfreq), jnp.bfloat16),
            pltpu.VMEM((n, 8, LANES), jnp.float32),
            pltpu.VMEM((n, 8, LANES), jnp.float32),
            pltpu.VMEM((nbins, n * 2 * LANES), jnp.bfloat16),
            pltpu.VMEM((n * 2 * LANES, 2 * nfreq), jnp.bfloat16),
            pltpu.VMEM((n, BINS_DEV, 2 * nfreq), jnp.bfloat16),
            pltpu.VMEM((n, BINS_DEV, 2 * nfreq), jnp.bfloat16),
            dma((10,)),
            dma((n,)),
            dma((n,)),
            dma((n,)),
            dma((n,)),
            dma((n,)),
            dma((n,)),
        ],
        compiler_params=pltpu.CompilerParams(
            collective_id=0, has_side_effects=True, vmem_limit_bytes=60 * 1024 * 1024
        ),
    )(
        spectra,
        valid,
        partner,
        pair_bin,
        pair_count,
        jnp.asarray(expanders(nchan, nwin)),
        jnp.asarray(base_table(nfreq)),
        jnp.asarray(slice_phases(n, nfreq, scale)),
    )


def solution(mesh):
    in_specs = (
        P(("grp", "chan"), None, None, None),
        P(("grp", "chan"), None),
        P(),
        P(("grp", "chan")),
        P(("grp", "chan")),
    )
    out_specs = P(("grp", "chan"), None)
    whole_bands = F % (mesh.shape["chan"] * BAND) == 0
    return jax.shard_map(
        on_device_slices if whole_bands else on_device_blocks,
        mesh=mesh,
        in_specs=in_specs,
        out_specs=out_specs,
        check_vma=False,
    )
```

```python
import functools
import math

import jax
import jax.numpy as jnp
import ml_dtypes
import numpy as np
from jax import lax
from jax.experimental import pallas as pl
from jax.experimental.pallas import tpu as pltpu
from jax.sharding import PartitionSpec as P

F = 4096
BAND = 128
LAGS = 1024
BINS_DEV = 8
PAIRS_DEV = 32
LANES = 128


def from_partner(block, axis, bit):
    count = lax.axis_size(axis)
    route = []
    for low in range(count):
        high = low | 1 << bit
        if high != low and high < count:
            route += [(low, high), (high, low)]
    return lax.ppermute(block, axis, route)


def whiten(spectra, valid):
    values = spectra.astype(jnp.float32)
    power = values[:, :, 0] * values[:, :, 0] + values[:, :, 1] * values[:, :, 1]
    nchan, nwin, nfreq = power.shape
    banded = jnp.mean(power.reshape(nchan, nwin, nfreq // BAND, BAND), axis=-1)
    amplitude = jnp.repeat(jnp.sqrt(banded + 1e-06), BAND, axis=-1)
    weights = valid.astype(jnp.float32)[:, :, None, None]
    return (values * weights / amplitude[:, :, None, :]).astype(jnp.bfloat16)


def lag_table():
    freqs = jnp.arange(F, dtype=jnp.int32)
    shifts = jnp.arange(LAGS, dtype=jnp.int32) - LAGS // 2
    phase = jnp.mod(freqs[:, None] * shifts[None, :], 2 * F)
    angle = phase.astype(jnp.float32) * (2.0 * math.pi / (2 * F))
    scale = 1.0 / math.sqrt(F)
    return jnp.concatenate([jnp.cos(angle) * scale, -jnp.sin(angle) * scale], axis=0).astype(
        jnp.bfloat16
    )


def cross_product(left_part, right_part):
    return jnp.einsum("awf,bwf->abf", left_part, right_part, preferred_element_type=jnp.float32)


def correlate(own_block, other_block, table):
    own_real = own_block[:, :, 0]
    own_imag = own_block[:, :, 1]
    oth_real = other_block[:, :, 0]
    oth_imag = other_block[:, :, 1]
    real_part = cross_product(own_real, oth_real) + cross_product(own_imag, oth_imag)
    imag_part = cross_product(own_imag, oth_real) - cross_product(own_real, oth_imag)
    nchan = own_block.shape[0]
    nwin = own_block.shape[1]
    spec = (jnp.concatenate([real_part, imag_part], axis=-1) * (1.0 / nwin)).reshape(
        nchan * nchan, -1
    )
    spec = spec.astype(jnp.bfloat16)
    return jnp.dot(spec, table, preferred_element_type=jnp.float32)


def select_sum(selector, corr_high, corr_low):
    return jnp.dot(selector, corr_high, preferred_element_type=jnp.float32) + jnp.dot(
        selector, corr_low, preferred_element_type=jnp.float32
    )


def on_device_blocks(spectra, valid, partner, pair_bin, pair_count):
    white = whiten(spectra, valid)
    nblocks = lax.axis_size("chan")
    round_mask = partner[0]
    paired = white
    for bit_index in range(nblocks.bit_length() - 1):
        swapped = from_partner(paired, "chan", bit_index)
        paired = jnp.where(round_mask >> bit_index & 1 == 1, swapped, paired)
    table = lag_table()
    self_corr = correlate(white, white, table)
    cross_corr = correlate(white, paired, table)
    corr = jnp.concatenate([self_corr, cross_corr], axis=0)
    corr_high = corr.astype(jnp.bfloat16)
    corr_low = (corr - corr_high.astype(jnp.float32)).astype(jnp.bfloat16)
    rows = jnp.arange(corr.shape[0], dtype=jnp.int32)
    live_rows = (rows < pair_count[0]) & (pair_bin >= 0)
    kept_bins = jnp.where(live_rows, pair_bin, -1)
    targets = lax.iota(jnp.int32, nblocks * BINS_DEV)
    selector = (kept_bins[None, :] == targets[:, None]).astype(jnp.bfloat16)
    terms = select_sum(selector, corr_high, corr_low).reshape(nblocks, BINS_DEV, -1)
    received = lax.all_to_all(terms, "chan", split_axis=0, concat_axis=0, tiled=True)
    summed = jnp.sum(received, axis=0)
    return summed * (1.0 / math.sqrt(PAIRS_DEV // BINS_DEV))


def base_table(nfreq):
    shifts = np.arange(LAGS) - LAGS // 2
    angle = np.mod(np.arange(nfreq)[:, None] * shifts[None, :], 2 * F) * (2.0 * math.pi / (2 * F))
    cos, sin = np.cos(angle), np.sin(angle)
    return np.concatenate(
        [np.concatenate([cos, sin], axis=1), np.concatenate([-sin, cos], axis=1)], axis=0
    ).astype(ml_dtypes.bfloat16)


def slice_phases(nslices, nfreq, scale):
    shifts = np.arange(LAGS) - LAGS // 2
    first = np.arange(nslices) * nfreq
    angle = np.mod(first[:, None] * shifts[None, :], 2 * F) * (2.0 * math.pi / (2 * F))
    both = np.concatenate([np.cos(angle), -np.sin(angle)], axis=1) * scale
    return both.astype(np.float32)[:, None, :]


def expanders(nchan, nwin):
    row = np.arange(LANES)
    per_chan = 2 * nwin
    step = row // (nchan * per_chan)
    first = row // per_chan % nchan
    window = row // 2 % nwin
    second = (first + step) % nchan
    nvalid = nchan * nwin
    pair = first * nchan + second
    lanes = (
        nvalid + pair,
        nvalid + nchan * nchan + pair,
        first * nwin + window,
        second * nwin + window,
    )
    return np.concatenate(
        [(np.arange(LANES)[:, None] == lane[None, :]) for lane in lanes], axis=1
    ).astype(ml_dtypes.bfloat16)


def swap_pairs(rows):
    size = rows.shape[-2]
    axis = rows.ndim - 2
    even = lax.broadcasted_iota(jnp.int32, rows.shape, axis) % 2 == 0
    return jnp.where(
        even, pltpu.roll(rows, size - 1, axis), pltpu.roll(rows, 1, axis)
    ), even


def kernel(
    dims,
    spectra_ref,
    valid_hbm,
    partner_hbm,
    bin_hbm,
    count_hbm,
    expand_hbm,
    table_hbm,
    phase_hbm,
    out_ref,
    valid_ref,
    partner_ref,
    bin_ref,
    count_ref,
    expand_ref,
    meta_ref,
    raw,
    metas,
    table,
    phases,
    rolled,
    turned,
    kept,
    other_valid,
    selector,
    products,
    outgoing,
    incoming,
    local_sems,
    send_a,
    recv_a,
    send_m,
    recv_m,
    send_b,
    recv_b,
):
    n, nchan, nwin, nfreq, nbins_dev = dims
    nrow = nchan * nwin * 2
    nbins = n * nbins_dev
    me = lax.axis_index("chan")
    copy_table = pltpu.make_async_copy(table_hbm, table, local_sems.at[0])
    copy_phase = pltpu.make_async_copy(phase_hbm, phases, local_sems.at[1])

    def mine(target):
        return pl.ds(pl.multiple_of(target * nfreq, nfreq), nfreq)

    own_raw = pltpu.make_async_copy(
        spectra_ref.at[:, :, :, mine(me)], raw.at[me], local_sems.at[2]
    )
    own_meta = pltpu.make_async_copy(meta_ref, metas.at[me], local_sems.at[3])
    small = [
        pltpu.make_async_copy(src, dst, local_sems.at[5 + i])
        for i, (src, dst) in enumerate(
            (
                (valid_hbm, valid_ref),
                (bin_hbm, bin_ref),
                (count_hbm, count_ref),
                (partner_hbm, partner_ref),
                (expand_hbm, expand_ref),
            )
        )
    ]
    for copy in small:
        copy.start()

    def peer(k):
        bits = range((n - 1).bit_length())
        return sum((me // 2**b + k // 2**b) % 2 * 2**b for b in bits)

    barrier = pltpu.get_barrier_semaphore()
    for k in range(1, n):
        pl.semaphore_signal(
            barrier,
            inc=1,
            device_id={"chan": peer(k)},
            device_id_type=pl.DeviceIdType.MESH,
        )
    own_raw.start()
    copy_table.start()
    copy_phase.start()
    for copy in small:
        copy.wait()
    lane = lax.broadcasted_iota(jnp.int32, metas.shape[1:], 1)
    meta = jnp.full(metas.shape[1:], count_ref[0], jnp.int32)
    for c in range(nchan):
        for w in range(nwin):
            meta = jnp.where(lane == c * nwin + w, valid_ref[c, w], meta)
    for row in range(2 * nchan * nchan):
        meta = jnp.where(lane == nchan * nwin + row, bin_ref[row], meta)
    meta_ref[...] = meta
    pl.semaphore_wait(barrier, n - 1)
    own_meta.start()

    def remote(src, dst, send, recv, target):
        return pltpu.make_async_remote_copy(
            src_ref=src,
            dst_ref=dst,
            send_sem=send,
            recv_sem=recv,
            device_id={"chan": target},
            device_id_type=pl.DeviceIdType.MESH,
        )

    def meta_copy(k, source):
        return remote(
            meta_ref, metas.at[source], send_m.at[k], recv_m.at[k], peer(k)
        )

    def raw_copy(k, source):
        target = peer(k)
        return remote(
            spectra_ref.at[:, :, :, mine(target)], raw.at[source], send_a.at[k], recv_a.at[k], target
        )

    order = range(n - 1, 0, -1)
    for k in order:
        meta_copy(k, me).start()
    for k in order:
        raw_copy(k, me).start()

    own_meta.wait()
    for k in range(1, n):
        meta_copy(k, peer(k)).wait_recv()
    values = metas[:, 0, :]
    lane = lax.broadcasted_iota(jnp.int32, (n, LANES), 1)
    nvalid = nchan * nwin
    npairs = 2 * nchan * nchan
    is_count = lane == nvalid + npairs
    count = jnp.sum(jnp.where(is_count, values, 0), axis=1, keepdims=True)
    is_pair = (lane >= nvalid) & (lane < nvalid + npairs)
    dropped = is_pair & ((lane - nvalid >= count) | (values < 0))
    values = jnp.where(dropped, -1, jnp.where(is_count, 0, values))
    spread = jnp.dot(
        values.astype(jnp.float32).astype(jnp.bfloat16),
        expand_ref[...],
        preferred_element_type=jnp.float32,
    )
    self_bin = spread[:, :LANES]
    cross_bin = spread[:, LANES : 2 * LANES]
    first_ok = spread[:, 2 * LANES : 3 * LANES] > 0.5
    second_valid = spread[:, 3 * LANES :]
    self_bin = jnp.where(first_ok & (second_valid > 0.5), self_bin, -1.0)
    cross_bin = jnp.where(first_ok, cross_bin, -1.0)
    for p in range(n):
        kept[p, 0:1, :] = self_bin[p : p + 1]
        kept[p, 1:2, :] = cross_bin[p : p + 1]
        other_valid[p, 0:1, :] = second_valid[p : p + 1]

    bin_rows = lax.broadcasted_iota(jnp.int32, (nbins, LANES), 0).astype(jnp.float32)

    def select(p, carry):
        other = other_valid[partner_ref[p], 0:1, :]
        crossing = jnp.where(other > 0.5, kept[p, 1:2, :], -1.0)
        at = pl.multiple_of(p * 2 * LANES, 2 * LANES)
        own = kept[p, 0:1, :]
        selector[:, pl.ds(at, LANES)] = jnp.where(bin_rows == own, 1.0, 0.0).astype(jnp.bfloat16)
        selector[:, pl.ds(at + LANES, LANES)] = jnp.where(bin_rows == crossing, 1.0, 0.0).astype(
            jnp.bfloat16
        )
        return carry

    lax.fori_loop(0, n, select, 0)

    def prepare(p):
        x = raw[p].astype(jnp.float32).reshape(nchan, 2 * nwin, nfreq)
        swapped, even = swap_pairs(x)
        power = x * x + swapped * swapped
        scales = []
        for b in range(nfreq // BAND):
            total = jnp.sum(power[:, :, b * BAND : (b + 1) * BAND], axis=-1, keepdims=True)
            scale = lax.rsqrt(total * (1.0 / BAND) + 1e-06)
            scales.append(jnp.broadcast_to(scale, (nchan, 2 * nwin, BAND)))
        scale = jnp.concatenate(scales, axis=-1)
        white = x * scale
        turn = jnp.where(even, -swapped, swapped) * scale
        for s in range(nchan):
            at = s * nrow
            part = jnp.concatenate([white[s:], white[:s]], axis=0) if s else white
            rolled[p, at : at + nrow, :] = part.reshape(nrow, nfreq).astype(jnp.bfloat16)
            part = jnp.concatenate([turn[s:], turn[:s]], axis=0) if s else turn
            turned[p, at : at + nrow, :] = part.reshape(nrow, nfreq).astype(jnp.bfloat16)

    own_raw.wait()
    prepare(me)

    def arrive(i, carry):
        k = lax.rem(i, n)
        source = peer(k)
        raw_copy(k, source).wait_recv()
        prepare(source)
        return carry

    lax.fori_loop(1, n, arrive, 0)

    def multiply(p, carry):
        q = partner_ref[p]
        x = rolled[p, 0:nrow, :]
        at = pl.multiple_of(p * 2 * LANES, 2 * LANES)
        for s in range(nchan):
            here = slice(s * nrow, (s + 1) * nrow)
            mid = at + s * nrow
            products[pl.ds(mid, nrow), 0:nfreq] = x * rolled[p, here, :]
            products[pl.ds(mid, nrow), nfreq : 2 * nfreq] = x * turned[p, here, :]
            products[pl.ds(mid + LANES, nrow), 0:nfreq] = x * rolled[q, here, :]
            products[pl.ds(mid + LANES, nrow), nfreq : 2 * nfreq] = x * turned[q, here, :]
        return carry

    lax.fori_loop(0, n, multiply, 0)

    terms = jnp.dot(selector[...], products[...], preferred_element_type=jnp.float32)
    outgoing[...] = terms.reshape(n, nbins_dev, 2 * nfreq).astype(jnp.bfloat16)

    def term_copy(k, source):
        target = peer(k)
        return remote(
            outgoing.at[target], incoming.at[source], send_b.at[k], recv_b.at[k], target
        )

    own_terms = pltpu.make_async_copy(outgoing.at[me], incoming.at[me], local_sems.at[4])
    for k in order:
        term_copy(k, me).start()
    own_terms.start()
    copy_table.wait()
    copy_phase.wait()
    own_terms.wait()
    for k in range(1, n):
        term_copy(k, peer(k)).wait_recv()

    stacked = incoming[...].astype(jnp.float32).reshape(nbins, 2 * nfreq).astype(jnp.bfloat16)
    lags = jnp.dot(stacked, table[...], preferred_element_type=jnp.float32)
    lags = jnp.sum(lags.reshape(n, nbins_dev, 2 * LAGS) * phases[...], axis=0)
    out_ref[...] = lags[:, :LAGS] + lags[:, LAGS:]

    for k in range(1, n):
        meta_copy(k, me).wait_send()
        raw_copy(k, me).wait_send()
        term_copy(k, me).wait_send()


def on_device_slices(spectra, valid, partner, pair_bin, pair_count):
    n = lax.axis_size("chan")
    nchan, nwin, _, nfreq_all = spectra.shape
    nfreq = nfreq_all // n
    nrow = nchan * nwin * 2
    nbins = n * BINS_DEV
    scale = 1.0 / (math.sqrt(nfreq_all) * nwin * math.sqrt(PAIRS_DEV // BINS_DEV))
    hbm = pl.BlockSpec(memory_space=pltpu.HBM)
    vmem = pl.BlockSpec(memory_space=pltpu.VMEM)
    dma = pltpu.SemaphoreType.DMA
    return pl.pallas_call(
        functools.partial(kernel, (n, nchan, nwin, nfreq, BINS_DEV)),
        out_shape=jax.ShapeDtypeStruct((BINS_DEV, LAGS), jnp.float32),
        in_specs=[hbm] * 8,
        out_specs=vmem,
        scratch_shapes=[
            pltpu.SMEM(valid.shape, jnp.int32),
            pltpu.SMEM(partner.shape, jnp.int32),
            pltpu.SMEM(pair_bin.shape, jnp.int32),
            pltpu.SMEM(pair_count.shape, jnp.int32),
            pltpu.VMEM((LANES, 4 * LANES), jnp.bfloat16),
            pltpu.VMEM((8, LANES), jnp.int32),
            pltpu.VMEM((n, nchan, nwin, 2, nfreq), jnp.bfloat16),
            pltpu.VMEM((n, 8, LANES), jnp.int32),
            pltpu.VMEM((2 * nfreq, 2 * LAGS), jnp.bfloat16),
            pltpu.VMEM((n, 1, 2 * LAGS), jnp.float32),
            pltpu.VMEM((n, nchan * nrow, nfreq), jnp.bfloat16),
            pltpu.VMEM((n, nchan * nrow, nfreq), jnp.bfloat16),
            pltpu.VMEM((n, 8, LANES), jnp.float32),
            pltpu.VMEM((n, 8, LANES), jnp.float32),
            pltpu.VMEM((nbins, n * 2 * LANES), jnp.bfloat16),
            pltpu.VMEM((n * 2 * LANES, 2 * nfreq), jnp.bfloat16),
            pltpu.VMEM((n, BINS_DEV, 2 * nfreq), jnp.bfloat16),
            pltpu.VMEM((n, BINS_DEV, 2 * nfreq), jnp.bfloat16),
            dma((10,)),
            dma((n,)),
            dma((n,)),
            dma((n,)),
            dma((n,)),
            dma((n,)),
            dma((n,)),
        ],
        compiler_params=pltpu.CompilerParams(
            collective_id=0, has_side_effects=True, vmem_limit_bytes=60 * 1024 * 1024
        ),
    )(
        spectra,
        valid,
        partner,
        pair_bin,
        pair_count,
        jnp.asarray(expanders(nchan, nwin)),
        jnp.asarray(base_table(nfreq)),
        jnp.asarray(slice_phases(n, nfreq, scale)),
    )


def solution(mesh):
    in_specs = (
        P(("grp", "chan"), None, None, None),
        P(("grp", "chan"), None),
        P(),
        P(("grp", "chan")),
        P(("grp", "chan")),
    )
    out_specs = P(("grp", "chan"), None)
    whole_bands = F % (mesh.shape["chan"] * BAND) == 0
    return jax.shard_map(
        on_device_slices if whole_bands else on_device_blocks,
        mesh=mesh,
        in_specs=in_specs,
        out_specs=out_specs,
        check_vma=False,
    )
```

```python
import functools
import math

import jax
import jax.numpy as jnp
import ml_dtypes
import numpy as np
from jax import lax
from jax.experimental import pallas as pl
from jax.experimental.pallas import tpu as pltpu
from jax.sharding import PartitionSpec as P

F = 4096
BAND = 128
LAGS = 1024
BINS_DEV = 8
PAIRS_DEV = 32
LANES = 128
GROUP = 4


def from_partner(block, axis, bit):
    count = lax.axis_size(axis)
    route = []
    for low in range(count):
        high = low | 1 << bit
        if high != low and high < count:
            route += [(low, high), (high, low)]
    return lax.ppermute(block, axis, route)


def whiten(spectra, valid):
    values = spectra.astype(jnp.float32)
    power = values[:, :, 0] * values[:, :, 0] + values[:, :, 1] * values[:, :, 1]
    nchan, nwin, nfreq = power.shape
    banded = jnp.mean(power.reshape(nchan, nwin, nfreq // BAND, BAND), axis=-1)
    amplitude = jnp.repeat(jnp.sqrt(banded + 1e-06), BAND, axis=-1)
    weights = valid.astype(jnp.float32)[:, :, None, None]
    return (values * weights / amplitude[:, :, None, :]).astype(jnp.bfloat16)


def lag_table():
    freqs = jnp.arange(F, dtype=jnp.int32)
    shifts = jnp.arange(LAGS, dtype=jnp.int32) - LAGS // 2
    phase = jnp.mod(freqs[:, None] * shifts[None, :], 2 * F)
    angle = phase.astype(jnp.float32) * (2.0 * math.pi / (2 * F))
    scale = 1.0 / math.sqrt(F)
    return jnp.concatenate([jnp.cos(angle) * scale, -jnp.sin(angle) * scale], axis=0).astype(
        jnp.bfloat16
    )


def cross_product(left_part, right_part):
    return jnp.einsum("awf,bwf->abf", left_part, right_part, preferred_element_type=jnp.float32)


def correlate(own_block, other_block, table):
    own_real = own_block[:, :, 0]
    own_imag = own_block[:, :, 1]
    oth_real = other_block[:, :, 0]
    oth_imag = other_block[:, :, 1]
    real_part = cross_product(own_real, oth_real) + cross_product(own_imag, oth_imag)
    imag_part = cross_product(own_imag, oth_real) - cross_product(own_real, oth_imag)
    nchan = own_block.shape[0]
    nwin = own_block.shape[1]
    spec = (jnp.concatenate([real_part, imag_part], axis=-1) * (1.0 / nwin)).reshape(
        nchan * nchan, -1
    )
    spec = spec.astype(jnp.bfloat16)
    return jnp.dot(spec, table, preferred_element_type=jnp.float32)


def select_sum(selector, corr_high, corr_low):
    return jnp.dot(selector, corr_high, preferred_element_type=jnp.float32) + jnp.dot(
        selector, corr_low, preferred_element_type=jnp.float32
    )


def on_device_blocks(spectra, valid, partner, pair_bin, pair_count):
    white = whiten(spectra, valid)
    nblocks = lax.axis_size("chan")
    round_mask = partner[0]
    paired = white
    for bit_index in range(nblocks.bit_length() - 1):
        swapped = from_partner(paired, "chan", bit_index)
        paired = jnp.where(round_mask >> bit_index & 1 == 1, swapped, paired)
    table = lag_table()
    self_corr = correlate(white, white, table)
    cross_corr = correlate(white, paired, table)
    corr = jnp.concatenate([self_corr, cross_corr], axis=0)
    corr_high = corr.astype(jnp.bfloat16)
    corr_low = (corr - corr_high.astype(jnp.float32)).astype(jnp.bfloat16)
    rows = jnp.arange(corr.shape[0], dtype=jnp.int32)
    live_rows = (rows < pair_count[0]) & (pair_bin >= 0)
    kept_bins = jnp.where(live_rows, pair_bin, -1)
    targets = lax.iota(jnp.int32, nblocks * BINS_DEV)
    selector = (kept_bins[None, :] == targets[:, None]).astype(jnp.bfloat16)
    terms = select_sum(selector, corr_high, corr_low).reshape(nblocks, BINS_DEV, -1)
    received = lax.all_to_all(terms, "chan", split_axis=0, concat_axis=0, tiled=True)
    summed = jnp.sum(received, axis=0)
    return summed * (1.0 / math.sqrt(PAIRS_DEV // BINS_DEV))


def base_table(nfreq):
    shifts = np.arange(LAGS) - LAGS // 2
    angle = np.mod(np.arange(nfreq)[:, None] * shifts[None, :], 2 * F) * (2.0 * math.pi / (2 * F))
    cos, sin = np.cos(angle), np.sin(angle)
    return np.concatenate(
        [np.concatenate([cos, sin], axis=1), np.concatenate([-sin, cos], axis=1)], axis=0
    ).astype(ml_dtypes.bfloat16)


def slice_phases(nslices, nfreq, scale):
    shifts = np.arange(LAGS) - LAGS // 2
    first = np.arange(nslices) * nfreq
    angle = np.mod(first[:, None] * shifts[None, :], 2 * F) * (2.0 * math.pi / (2 * F))
    both = np.concatenate([np.cos(angle), -np.sin(angle)], axis=1) * scale
    return both.astype(np.float32)[:, None, :]


def expanders(nchan, nwin):
    row = np.arange(LANES)
    per_chan = 2 * nwin
    step = row // (nchan * per_chan)
    first = row // per_chan % nchan
    window = row // 2 % nwin
    second = (first + step) % nchan
    nvalid = nchan * nwin
    pair = first * nchan + second
    lanes = (
        nvalid + pair,
        nvalid + nchan * nchan + pair,
        first * nwin + window,
        second * nwin + window,
    )
    return np.concatenate(
        [(np.arange(LANES)[:, None] == lane[None, :]) for lane in lanes], axis=1
    ).astype(ml_dtypes.bfloat16)


def swap_pairs(rows):
    size = rows.shape[-2]
    axis = rows.ndim - 2
    even = lax.broadcasted_iota(jnp.int32, rows.shape, axis) % 2 == 0
    return jnp.where(
        even, pltpu.roll(rows, size - 1, axis), pltpu.roll(rows, 1, axis)
    ), even


def kernel(
    dims,
    spectra_ref,
    valid_hbm,
    partner_hbm,
    bin_hbm,
    count_hbm,
    expand_hbm,
    table_hbm,
    phase_hbm,
    out_ref,
    valid_ref,
    partner_ref,
    bin_ref,
    count_ref,
    expand_ref,
    meta_ref,
    raw,
    metas,
    table,
    phases,
    rolled,
    turned,
    kept,
    other_valid,
    selector,
    products,
    self_selector,
    spread_selector,
    self_products,
    totals,
    outgoing,
    incoming,
    local_sems,
    send_a,
    recv_a,
    send_m,
    recv_m,
    send_b,
    recv_b,
):
    n, nchan, nwin, nfreq, nbins_dev = dims
    nrow = nchan * nwin * 2
    nbins = n * nbins_dev
    me = lax.axis_index("chan")
    copy_table = pltpu.make_async_copy(table_hbm, table, local_sems.at[0])
    copy_phase = pltpu.make_async_copy(phase_hbm, phases, local_sems.at[1])

    def mine(target):
        return pl.ds(pl.multiple_of(target * nfreq, nfreq), nfreq)

    own_raw = pltpu.make_async_copy(
        spectra_ref.at[:, :, :, mine(me)], raw.at[me], local_sems.at[2]
    )
    own_meta = pltpu.make_async_copy(meta_ref, metas.at[me], local_sems.at[3])
    small = [
        pltpu.make_async_copy(src, dst, local_sems.at[5 + i])
        for i, (src, dst) in enumerate(
            (
                (valid_hbm, valid_ref),
                (bin_hbm, bin_ref),
                (count_hbm, count_ref),
                (partner_hbm, partner_ref),
                (expand_hbm, expand_ref),
            )
        )
    ]
    for copy in small:
        copy.start()

    def peer(k):
        bits = range((n - 1).bit_length())
        return sum((me // 2**b + k // 2**b) % 2 * 2**b for b in bits)

    barrier = pltpu.get_barrier_semaphore()
    for k in range(1, n):
        pl.semaphore_signal(
            barrier,
            inc=1,
            device_id={"chan": peer(k)},
            device_id_type=pl.DeviceIdType.MESH,
        )
    own_raw.start()
    copy_table.start()
    copy_phase.start()
    for copy in small:
        copy.wait()
    lane = lax.broadcasted_iota(jnp.int32, metas.shape[1:], 1)
    meta = jnp.full(metas.shape[1:], count_ref[0], jnp.int32)
    for c in range(nchan):
        for w in range(nwin):
            meta = jnp.where(lane == c * nwin + w, valid_ref[c, w], meta)
    for row in range(2 * nchan * nchan):
        meta = jnp.where(lane == nchan * nwin + row, bin_ref[row], meta)
    meta_ref[...] = meta
    pl.semaphore_wait(barrier, n - 1)
    own_meta.start()

    def remote(src, dst, send, recv, target):
        return pltpu.make_async_remote_copy(
            src_ref=src,
            dst_ref=dst,
            send_sem=send,
            recv_sem=recv,
            device_id={"chan": target},
            device_id_type=pl.DeviceIdType.MESH,
        )

    def meta_copy(k, source):
        return remote(
            meta_ref, metas.at[source], send_m.at[k], recv_m.at[k], peer(k)
        )

    def raw_copy(k, source):
        target = peer(k)
        return remote(
            spectra_ref.at[:, :, :, mine(target)], raw.at[source], send_a.at[k], recv_a.at[k], target
        )

    order = range(n - 1, 0, -1)
    for k in order:
        meta_copy(k, me).start()
    for k in order:
        raw_copy(k, me).start()

    own_meta.wait()
    for k in range(1, n):
        meta_copy(k, peer(k)).wait_recv()
    values = metas[:, 0, :]
    lane = lax.broadcasted_iota(jnp.int32, (n, LANES), 1)
    nvalid = nchan * nwin
    npairs = 2 * nchan * nchan
    is_count = lane == nvalid + npairs
    count = jnp.sum(jnp.where(is_count, values, 0), axis=1, keepdims=True)
    is_pair = (lane >= nvalid) & (lane < nvalid + npairs)
    dropped = is_pair & ((lane - nvalid >= count) | (values < 0))
    values = jnp.where(dropped, -1, jnp.where(is_count, 0, values))
    spread = jnp.dot(
        values.astype(jnp.float32).astype(jnp.bfloat16),
        expand_ref[...],
        preferred_element_type=jnp.float32,
    )
    self_bin = spread[:, :LANES]
    cross_bin = spread[:, LANES : 2 * LANES]
    first_ok = spread[:, 2 * LANES : 3 * LANES] > 0.5
    second_valid = spread[:, 3 * LANES :]
    self_bin = jnp.where(first_ok & (second_valid > 0.5), self_bin, -1.0)
    cross_bin = jnp.where(first_ok, cross_bin, -1.0)
    for p in range(n):
        kept[p, 0:1, :] = self_bin[p : p + 1]
        kept[p, 1:2, :] = cross_bin[p : p + 1]
        other_valid[p, 0:1, :] = second_valid[p : p + 1]

    bin_rows = lax.broadcasted_iota(jnp.int32, (nbins, LANES), 0).astype(jnp.float32)

    def select(p, carry):
        other = other_valid[partner_ref[p], 0:1, :]
        crossing = jnp.where(other > 0.5, kept[p, 1:2, :], -1.0)
        at = pl.multiple_of(p * LANES, LANES)
        own = kept[p, 0:1, :]
        self_selector[p] = jnp.where(bin_rows == own, 1.0, 0.0).astype(jnp.bfloat16)
        selector[:, pl.ds(at, LANES)] = jnp.where(bin_rows == crossing, 1.0, 0.0).astype(
            jnp.bfloat16
        )
        return carry

    lax.fori_loop(0, n, select, 0)

    def prepare(p):
        x = raw[p].astype(jnp.float32).reshape(nchan, 2 * nwin, nfreq)
        swapped, even = swap_pairs(x)
        power = x * x + swapped * swapped
        scales = []
        for b in range(nfreq // BAND):
            total = jnp.sum(power[:, :, b * BAND : (b + 1) * BAND], axis=-1, keepdims=True)
            scale = lax.rsqrt(total * (1.0 / BAND) + 1e-06)
            scales.append(jnp.broadcast_to(scale, (nchan, 2 * nwin, BAND)))
        scale = jnp.concatenate(scales, axis=-1)
        white = x * scale
        turn = jnp.where(even, -swapped, swapped) * scale
        for s in range(nchan):
            at = s * nrow
            part = jnp.concatenate([white[s:], white[:s]], axis=0) if s else white
            rolled[p, at : at + nrow, :] = part.reshape(nrow, nfreq).astype(jnp.bfloat16)
            part = jnp.concatenate([turn[s:], turn[:s]], axis=0) if s else turn
            turned[p, at : at + nrow, :] = part.reshape(nrow, nfreq).astype(jnp.bfloat16)

    def multiply_self(p, slot):
        x = rolled[p, 0:nrow, :]
        for s in range(nchan):
            here = slice(s * nrow, (s + 1) * nrow)
            rows = slice(slot * LANES + s * nrow, slot * LANES + (s + 1) * nrow)
            self_products[rows, 0:nfreq] = x * rolled[p, here, :]
            self_products[rows, nfreq : 2 * nfreq] = x * turned[p, here, :]

    totals[...] = jnp.zeros_like(totals)

    def add_group(members):
        for slot, p in enumerate(members):
            multiply_self(p, slot)
            spread_selector[:, slot * LANES : (slot + 1) * LANES] = self_selector[p]
        totals[...] += jnp.dot(
            spread_selector[...], self_products[...], preferred_element_type=jnp.float32
        )

    arrival = list(range(n // 2)) + list(range(n - 1, n // 2 - 1, -1))
    for g in range(0, n, GROUP):
        members = [peer(k) for k in arrival[g : g + GROUP]]
        for k, source in zip(arrival[g : g + GROUP], members):
            if k == 0:
                own_raw.wait()
            else:
                raw_copy(k, source).wait_recv()
            prepare(source)
        add_group(members)

    def multiply(p):
        q = partner_ref[p]
        x = rolled[p, 0:nrow, :]
        at = pl.multiple_of(p * LANES, LANES)
        for s in range(nchan):
            here = slice(s * nrow, (s + 1) * nrow)
            mid = at + s * nrow
            products[pl.ds(mid, nrow), 0:nfreq] = x * rolled[q, here, :]
            products[pl.ds(mid, nrow), nfreq : 2 * nfreq] = x * turned[q, here, :]

    def multiply_four(i, carry):
        for j in range(4):
            multiply(4 * i + j)
        return carry

    lax.fori_loop(0, n // 4, multiply_four, 0)

    terms = totals[...] + jnp.dot(
        selector[...], products[...], preferred_element_type=jnp.float32
    )
    outgoing[...] = terms.reshape(n, nbins_dev, 2 * nfreq).astype(jnp.bfloat16)

    def term_copy(k, source):
        target = peer(k)
        return remote(
            outgoing.at[target], incoming.at[source], send_b.at[k], recv_b.at[k], target
        )

    own_terms = pltpu.make_async_copy(outgoing.at[me], incoming.at[me], local_sems.at[4])
    for k in order:
        term_copy(k, me).start()
    own_terms.start()
    copy_table.wait()
    copy_phase.wait()
    own_terms.wait()
    for k in range(1, n):
        term_copy(k, peer(k)).wait_recv()

    stacked = incoming[...].astype(jnp.float32).reshape(nbins, 2 * nfreq).astype(jnp.bfloat16)
    lags = jnp.dot(stacked, table[...], preferred_element_type=jnp.float32)
    lags = jnp.sum(lags.reshape(n, nbins_dev, 2 * LAGS) * phases[...], axis=0)
    out_ref[...] = lags[:, :LAGS] + lags[:, LAGS:]

    for k in range(1, n):
        meta_copy(k, me).wait_send()
        raw_copy(k, me).wait_send()
        term_copy(k, me).wait_send()


def on_device_slices(spectra, valid, partner, pair_bin, pair_count):
    n = lax.axis_size("chan")
    nchan, nwin, _, nfreq_all = spectra.shape
    nfreq = nfreq_all // n
    nrow = nchan * nwin * 2
    nbins = n * BINS_DEV
    scale = 1.0 / (math.sqrt(nfreq_all) * nwin * math.sqrt(PAIRS_DEV // BINS_DEV))
    hbm = pl.BlockSpec(memory_space=pltpu.HBM)
    vmem = pl.BlockSpec(memory_space=pltpu.VMEM)
    dma = pltpu.SemaphoreType.DMA
    return pl.pallas_call(
        functools.partial(kernel, (n, nchan, nwin, nfreq, BINS_DEV)),
        out_shape=jax.ShapeDtypeStruct((BINS_DEV, LAGS), jnp.float32),
        in_specs=[hbm] * 8,
        out_specs=vmem,
        scratch_shapes=[
            pltpu.SMEM(valid.shape, jnp.int32),
            pltpu.SMEM(partner.shape, jnp.int32),
            pltpu.SMEM(pair_bin.shape, jnp.int32),
            pltpu.SMEM(pair_count.shape, jnp.int32),
            pltpu.VMEM((LANES, 4 * LANES), jnp.bfloat16),
            pltpu.VMEM((1, LANES), jnp.int32),
            pltpu.VMEM((n, nchan, nwin, 2, nfreq), jnp.bfloat16),
            pltpu.VMEM((n, 1, LANES), jnp.int32),
            pltpu.VMEM((2 * nfreq, 2 * LAGS), jnp.bfloat16),
            pltpu.VMEM((n, 1, 2 * LAGS), jnp.float32),
            pltpu.VMEM((n, nchan * nrow, nfreq), jnp.bfloat16),
            pltpu.VMEM((n, nchan * nrow, nfreq), jnp.bfloat16),
            pltpu.VMEM((n, 8, LANES), jnp.float32),
            pltpu.VMEM((n, 8, LANES), jnp.float32),
            pltpu.VMEM((nbins, n * LANES), jnp.bfloat16),
            pltpu.VMEM((n * LANES, 2 * nfreq), jnp.bfloat16),
            pltpu.VMEM((n, nbins, LANES), jnp.bfloat16),
            pltpu.VMEM((nbins, GROUP * LANES), jnp.bfloat16),
            pltpu.VMEM((GROUP * LANES, 2 * nfreq), jnp.bfloat16),
            pltpu.VMEM((nbins, 2 * nfreq), jnp.float32),
            pltpu.VMEM((n, BINS_DEV, 2 * nfreq), jnp.bfloat16),
            pltpu.VMEM((n, BINS_DEV, 2 * nfreq), jnp.bfloat16),
            dma((10,)),
            dma((n,)),
            dma((n,)),
            dma((n,)),
            dma((n,)),
            dma((n,)),
            dma((n,)),
        ],
        compiler_params=pltpu.CompilerParams(
            collective_id=0, has_side_effects=True, vmem_limit_bytes=60 * 1024 * 1024
        ),
    )(
        spectra,
        valid,
        partner,
        pair_bin,
        pair_count,
        jnp.asarray(expanders(nchan, nwin)),
        jnp.asarray(base_table(nfreq)),
        jnp.asarray(slice_phases(n, nfreq, scale)),
    )


def solution(mesh):
    in_specs = (
        P(("grp", "chan"), None, None, None),
        P(("grp", "chan"), None),
        P(),
        P(("grp", "chan")),
        P(("grp", "chan")),
    )
    out_specs = P(("grp", "chan"), None)
    whole_bands = F % (mesh.shape["chan"] * BAND) == 0
    return jax.shard_map(
        on_device_slices if whole_bands else on_device_blocks,
        mesh=mesh,
        in_specs=in_specs,
        out_specs=out_specs,
        check_vma=False,
    )
```
